32 devices in a mesh: inst: 4 (over y, x), space: 8 (over z, core).
Axes of the slice: x: 2, y: 2, z: 4, core: 2. Of those that a mesh axis runs over, the one named last changes fastest.
Arguments:
- start_adjoint: float32 [32, 6, 64, 512], P('inst', None, 'space'), may hold values from -6 to 6
- adjoint_source: float32 [32, 6, 64, 512], P('inst', None, 'space'), may hold values from -48 to 48
- diagonal: float32 [6, 64, 512], P(None, 'space'), may hold values from 15 to 30
- flux_x: float32 [32, 6, 6, 64, 512], P('inst', None, None, 'space'), may hold values from -0.5 to 0.5
- flux_y: float32 [32, 6, 6, 64, 512], P('inst', None, None, 'space'), may hold values from -0.3 to 0.3
- shape_derivative: float32 [32, 6, 64, 512], P('inst', None, 'space'), may hold values from -6 to 6
- mode_basis: float32 [64, 512, 128], P('space'), may hold values from -0.0390625 to 0.0390625
- patch_of_cell: int32 [64, 512], P('space'), may hold values from 0 to 255, as said below
Outputs:
- adjoint: float32 [32, 6, 64, 512], P('inst', None, 'space')
- sensitivity: float32 [256, 128], P(('inst', 'space'))
The draws below stay inside these ranges and needn't reach their ends.
Inputs may be any that keep to these rules, and one draw needn't show every extreme that they name: `patch_of_cell`: patch index of each cell; a cell's patch lies within 16 patches of the one at its position in the order of cells (x slowest).
All inputs are finite; a program needn't handle non-finite values.
Results may differ from the reference program's by a relative error of at most 0.0001.
Values sent between devices are 32-bit elements; how exact they have to be, the bound alone decides.
No kernel may reach another device: no remote copies, remote signals or barrier semaphores. Data moves between devices by JAX's collectives and lax.ppermute only.
A program may use at most 128 MiB of HBM per device.

```python
import jax
import jax.numpy as jnp
from jax import lax

NT = 32
NV = 6
CX = 8
NY = 512
SWEEPS = 2
MODES = 128
PATCH_DEV = 8
NX = 64
NPATCH = 256
N_INST = 4


def draw_patch_of_cell(key, part):
    rows = jnp.arange(NX, dtype=jnp.int32)[:, None]
    cols = jnp.arange(NY, dtype=jnp.int32)[None, :]
    flat = rows * NY + cols
    base = flat * NPATCH // (NX * NY)
    offset = jax.random.randint(key, (NX, NY), -2 * PATCH_DEV, 2 * PATCH_DEV + 1, dtype=jnp.int32)
    ids = jnp.clip(base + offset, 0, NPATCH - 1)
    ids = ids.at[0, 0].set(0)
    ids = ids.at[NX - 1, NY - 1].set(NPATCH - 1)
    return ids.astype(jnp.int32)


def levels(stream_key, shape, cuts, smallest, top_value):
    def one(position, parts):
        steps = jax.random.uniform(jax.random.fold_in(jax.random.fold_in(stream_key, 6), position), (parts,), jnp.float32, smallest / len(cuts), top_value / len(cuts))
        return jnp.repeat(jnp.exp(steps), shape[position] // parts).reshape((-1,) + (1,) * (len(shape) - position - 1))

    level = one(*cuts[0])
    for cut in cuts[1:]:
        level = level * one(*cut)
    return level


def centred(stream_key, shape, spread, limit, split=(), held_as=jnp.bfloat16):
    factor_of = levels(stream_key, shape, split, -0.22, 0.18) if split else 1.0
    array = jax.random.normal(stream_key, shape, jnp.float32) * spread * factor_of
    return jnp.minimum(jnp.maximum(array, -limit), limit).astype(held_as)


def setup_inputs(seed: int = 0) -> dict:
    key_of = jax.random.split(jax.random.key(seed), 9)
    return {
        "start_adjoint": centred(key_of[0], (NT, NV, NX, NY), 1.0, 6.0, ((0, 4), (2, 8)), jnp.float32),
        "adjoint_source": centred(key_of[1], (NT, NV, NX, NY), 8.0, 48.0, ((0, 4), (2, 8)), jnp.float32),
        "diagonal": jnp.clip(15.0 + 15.0 * jax.random.uniform(key_of[2], (NV, NX, NY), jnp.float32) ** levels(key_of[2], (NV, NX, NY), ((1, 8),), -0.2, 0.2), 15.0, 30.0),
        "flux_x": jnp.clip(jax.random.uniform(key_of[3], (NT, NV, NV, NX, NY), jnp.float32, -0.5, 0.5) * levels(key_of[3], (NT, NV, NV, NX, NY), ((0, 4), (3, 8)), -0.4, 0.0), -0.5, 0.5),
        "flux_y": jnp.clip(jax.random.uniform(key_of[4], (NT, NV, NV, NX, NY), jnp.float32, -0.3, 0.3) * levels(key_of[4], (NT, NV, NV, NX, NY), ((0, 4), (3, 8)), -0.4, 0.0), -0.3, 0.3),
        "shape_derivative": centred(key_of[5], (NT, NV, NX, NY), 1.0, 6.0, ((0, 4), (2, 8)), jnp.float32),
        "mode_basis": centred(key_of[6], (NX, NY, MODES), (NT * NV * CX * NY // (PATCH_DEV * N_INST)) ** -0.5, 0.0390625, ((0, 8),), jnp.float32),
        "patch_of_cell": draw_patch_of_cell(jax.random.fold_in(key_of[8], 71), 0),
    }


spectral_scale = 0.1


def spectral_weights(offset):
    angles = (jnp.pi / NT) * offset.astype(jnp.float32)
    parity = 1.0 - 2.0 * jnp.remainder(offset, 2).astype(jnp.float32)
    nonzero = offset != 0
    sine_value = jnp.where(nonzero, jnp.sin(angles), 1.0)
    return jnp.where(nonzero, 0.5 * parity * jnp.cos(angles) / sine_value, 0.0)


def apply_operator(adjoint, plus_one, minus_one, plus_two, minus_two, spectral, diagonal, flux_x, flux_y):
    cell_above = jnp.pad(adjoint[..., 1:], ((0, 0), (0, 0), (0, 0), (0, 1)))
    cell_below = jnp.pad(adjoint[..., :-1], ((0, 0), (0, 0), (0, 0), (1, 0)))
    pitch_diff = (2.0 / 3.0) * (plus_one - minus_one) - (1.0 / 12.0) * (plus_two - minus_two)
    chord_diff = cell_above - cell_below
    transport = jnp.zeros_like(adjoint)
    for source in range(adjoint.shape[1]):
        transport = transport + flux_x[:, source] * pitch_diff[:, source:source + 1]
        transport = transport + flux_y[:, source] * chord_diff[:, source:source + 1]
    neighbours = plus_one + minus_one + cell_above + cell_below
    return diagonal[None] * adjoint - neighbours + transport + spectral_scale * spectral


def reference(start_adjoint, adjoint_source, diagonal, flux_x, flux_y, shape_derivative, mode_basis, patch_of_cell):
    instance_ids = jnp.arange(NT, dtype=jnp.int32)
    weights = spectral_weights(instance_ids[:, None] - instance_ids[None, :])
    adjoint = start_adjoint
    for repeat in range(SWEEPS):
        spectral = jnp.einsum('st,skxy->tkxy', weights, adjoint, precision=lax.Precision.HIGHEST)
        operated = apply_operator(adjoint, jnp.roll(adjoint, -1, 2), jnp.roll(adjoint, 1, 2),
                                  jnp.roll(adjoint, -2, 2), jnp.roll(adjoint, 2, 2),
                                  spectral, diagonal, flux_x, flux_y)
        adjoint = adjoint + (adjoint_source - operated) / diagonal[None]
    weight_sum = jnp.sum(adjoint * shape_derivative, axis=(0, 1))
    weighted = (mode_basis * weight_sum[:, :, None]).reshape(-1, MODES)
    sensitivity = jax.ops.segment_sum(weighted, patch_of_cell.reshape(-1), num_segments=NPATCH)
    return adjoint, sensitivity
```

```python
import math

import jax
import jax.numpy as jnp
import numpy as np
from jax import lax
from jax.experimental import pallas as pl
from jax.experimental.pallas import tpu as pltpu
from jax.sharding import PartitionSpec as P

NT = 32
PATCH_DEV = 8
REACH = 16
LANES = 128
SCALE = 0.1
F32 = jnp.float32


def weight_matrix(count):
    weights = np.zeros((count, count))
    for s in range(count):
        for t in range(count):
            if s != t:
                angle = math.pi * (s - t) / count
                weights[s, t] = 0.5 * (-1.0) ** (s - t) * math.cos(angle) / math.sin(angle)
    return weights


def circulant_apply(values):
    count = len(values)
    row = weight_matrix(count)[:, 0]
    if count == 2:
        return None
    half = count // 2
    total = [values[s] + values[s + half] for s in range(half)]
    diff = [values[s] - values[s + half] for s in range(half)]
    even = circulant_apply(total)
    q = [(row[d] - row[d + half]) / 2 for d in range(half)]
    quarter = half // 2

    def at(position):
        position %= count
        return (diff[position], 1.0) if position < half else (diff[position - half], -1.0)

    out = [None] * count
    for t in range(half):
        acc = None
        for d in range(1, quarter):
            plus, sign_plus = at(t + d)
            minus, sign_minus = at(t - d)
            pair = plus - minus if sign_plus == sign_minus else plus + minus
            term = float(q[d] * sign_plus) * pair
            acc = term if acc is None else acc + term
        last, sign = at(t + quarter)
        term = float(q[quarter] * sign) * last
        acc = term if acc is None else acc + term
        if even is None:
            out[t], out[t + half] = acc, -acc
        else:
            out[t], out[t + half] = even[t] + acc, even[t] - acc
    return out


def chunk_place(chunk, n_inst, ny):
    split = n_inst // (ny // LANES)
    return chunk // split, chunk % split


def lane_tile(index):
    return pl.ds(pl.multiple_of(index * LANES, LANES), LANES)


def pack_rows(row_block, first_row, ny):
    tiles = ny // LANES
    sub = lax.broadcasted_iota(jnp.int32, (8, LANES), 0)
    packed = None
    for y in range(tiles):
        tile = row_block[:, y * LANES : (y + 1) * LANES]
        shift = (2 * y - first_row) % 8
        moved = pltpu.roll(tile, shift, 0) if shift else tile
        packed = moved if packed is None else jnp.where(sub >= 2 * y, moved, packed)
    return packed


def pack_kernel(n_inst, a_ref, *refs):
    chunks, (first_ref, last_ref) = refs[:n_inst], refs[n_inst:]
    steps, nv, _, ny = a_ref.shape
    split = n_inst // (ny // LANES)
    part = nv // split
    me = lax.axis_index("inst")

    def at_step(t, _):
        for r in range(n_inst):
            y, v = chunk_place(me ^ r, n_inst, ny)
            for k in range(part):
                chunks[r][t, k] = a_ref[t, v * part + k, :, lane_tile(y)]
        for k in range(nv):
            rows = a_ref[t, k]
            first_ref[t, k] = pack_rows(rows, 0, ny)
            last_ref[t, k] = pack_rows(rows, 6, ny)
        return 0

    lax.fori_loop(0, steps, at_step, 0)


def local_terms(a_ref, prev_ref, next_ref, pitch, chord, near):
    nv, rows, ny = pitch.shape
    tiles = ny // LANES
    sub = lax.broadcasted_iota(jnp.int32, (rows, ny), 0)
    lane = lax.broadcasted_iota(jnp.int32, (rows, ny), 1)
    for k in range(nv):
        a = a_ref[0, k]
        before, after = prev_ref[0, k], next_ref[0, k]
        low = jnp.concatenate(
            [pltpu.roll(before, (-2 * y) % 8, 0) if y else before for y in range(tiles)], axis=1
        )
        high = jnp.concatenate(
            [pltpu.roll(after, 6 - 2 * y, 0) if y != 3 else after for y in range(tiles)], axis=1
        )
        edge = jnp.where(sub < 4, low, high)
        plus_two = jnp.where(sub >= 6, edge, pltpu.roll(a, 6, 0))
        plus_one = jnp.where(sub == 7, pltpu.roll(edge, 1, 0), pltpu.roll(a, 7, 0))
        minus_two = jnp.where(sub < 2, edge, pltpu.roll(a, 2, 0))
        minus_one = jnp.where(sub == 0, pltpu.roll(edge, 7, 0), pltpu.roll(a, 1, 0))
        above = jnp.where(lane == ny - 1, 0.0, pltpu.roll(a, ny - 1, 1))
        below = jnp.where(lane == 0, 0.0, pltpu.roll(a, 1, 1))
        pitch[k] = 2.0 / 3.0 * (plus_one - minus_one) - 1.0 / 12.0 * (plus_two - minus_two)
        chord[k] = above - below
        near[k] = plus_one + minus_one + above + below


def fresh_tile(k, y, src_ref, fx_ref, fy_ref, pitch_tiles, chord_tiles, near, inverse):
    lanes = slice(y * LANES, (y + 1) * LANES)
    acc = src_ref[0, k, :, lanes] + near[k, :, lanes]
    for j in range(len(pitch_tiles)):
        acc = acc - fx_ref[0, j, k, :, lanes] * pitch_tiles[j]
        acc = acc - fy_ref[0, j, k, :, lanes] * chord_tiles[j]
    return acc * inverse[k, :, lanes]


def first_sweep_kernel(
    n_inst, a_ref, prev_ref, next_ref, src_ref, d_ref, fx_ref, fy_ref, *refs
):
    out_refs, (whole, pitch, chord, near, inverse) = refs[:n_inst], refs[n_inst:]
    nv, _, ny = pitch.shape
    part = out_refs[0].shape[1]
    me = lax.axis_index("inst")

    @pl.when(pl.program_id(0) == 0)
    def _():
        inverse[...] = 1.0 / d_ref[...]

    local_terms(a_ref, prev_ref, next_ref, pitch, chord, near)
    for y in range(ny // LANES):
        lanes = slice(y * LANES, (y + 1) * LANES)
        pitch_tiles = [pitch[j, :, lanes] for j in range(nv)]
        chord_tiles = [chord[j, :, lanes] for j in range(nv)]
        for k in range(nv):
            whole[y * nv + k] = fresh_tile(
                k, y, src_ref, fx_ref, fy_ref, pitch_tiles, chord_tiles, near, inverse
            )
    for r in range(n_inst):
        base = (me ^ r) * part
        for k in range(part):
            out_refs[r][0, k] = whole[base + k]


def spectral_kernel(n_inst, second, d_ref, *refs):
    in_refs = refs[:n_inst]
    shift_refs = refs[n_inst : 2 * n_inst] if second else ()
    out_refs = refs[(2 if second else 1) * n_inst : (3 if second else 2) * n_inst]
    (work,) = refs[(3 if second else 2) * n_inst :]
    per, part = in_refs[0].shape[:2]
    ny = d_ref.shape[2]
    me = lax.axis_index("inst")
    y, v = chunk_place(me, n_inst, ny)

    def at_tile(c, _):
        for r in range(n_inst):
            base = (me ^ r) * per
            for t in range(per):
                value = in_refs[r][t, c]
                if second:
                    value = value - shift_refs[r][t, c]
                work[base + t] = value
        out = circulant_apply([work[s] for s in range(NT)])
        factor = SCALE / d_ref[v * part + c, :, lane_tile(y)]
        for s in range(NT):
            work[s] = out[s] * factor
        for r in range(n_inst):
            base = (me ^ r) * per
            for t in range(per):
                out_refs[r][t, c] = work[base + t]
        return 0

    lax.fori_loop(0, part, at_tile, 0)


def join_kernel(n_inst, *refs):
    b_refs, z_refs = refs[:n_inst], refs[n_inst : 2 * n_inst]
    a_ref, first_ref, last_ref = refs[2 * n_inst :]
    steps, nv, _, ny = a_ref.shape
    part = b_refs[0].shape[1]
    me = lax.axis_index("inst")

    def at_step(t, _):
        for r in range(n_inst):
            y, v = chunk_place(me ^ r, n_inst, ny)
            for k in range(part):
                a_ref[t, v * part + k, :, lane_tile(y)] = b_refs[r][t, k] - z_refs[r][t, k]
        for k in range(nv):
            rows = a_ref[t, k]
            first_ref[t, k] = pack_rows(rows, 0, ny)
            last_ref[t, k] = pack_rows(rows, 6, ny)
        return 0

    lax.fori_loop(0, steps, at_step, 0)


def second_sweep_kernel(
    a_ref, prev_ref, next_ref, src_ref, d_ref, fx_ref, fy_ref, shape_ref, out_ref, weight_ref,
    pitch, chord, near, inverse,
):
    nv, _, ny = pitch.shape

    @pl.when(pl.program_id(0) == 0)
    def _():
        inverse[...] = 1.0 / d_ref[...]
        weight_ref[...] = jnp.zeros_like(weight_ref)

    local_terms(a_ref, prev_ref, next_ref, pitch, chord, near)
    for y in range(ny // LANES):
        lanes = slice(y * LANES, (y + 1) * LANES)
        pitch_tiles = [pitch[j, :, lanes] for j in range(nv)]
        chord_tiles = [chord[j, :, lanes] for j in range(nv)]
        weight = weight_ref[:, lanes]
        for k in range(nv):
            value = fresh_tile(
                k, y, src_ref, fx_ref, fy_ref, pitch_tiles, chord_tiles, near, inverse
            )
            out_ref[0, k, :, lanes] = value
            weight = weight + value * shape_ref[0, k, :, lanes]
        weight_ref[:, lanes] = weight


def last_kernel(n_inst, x_ref, weight_ref, shape_ref, mode_ref, patch_ref, *refs):
    z_refs, (a_ref, send_ref, weight) = refs[:n_inst], refs[n_inst:]
    steps, nv, rows, ny = x_ref.shape
    part = z_refs[0].shape[1]
    me, space = lax.axis_index("inst"), lax.axis_index("space")
    owners = send_ref.shape[0]
    per_space = PATCH_DEV * n_inst
    window = per_space + 2 * REACH
    weight[...] = weight_ref[...]

    def at_step(t, _):
        for r in range(n_inst):
            y, v = chunk_place(me ^ r, n_inst, ny)
            total = jnp.zeros((rows, LANES), F32)
            for k in range(part):
                z = z_refs[r][t, k]
                a_ref[t, v * part + k, :, lane_tile(y)] = (
                    x_ref[t, v * part + k, :, lane_tile(y)] - z
                )
                total = total + z * shape_ref[t, v * part + k, :, lane_tile(y)]
            weight[:, lane_tile(y)] = weight[:, lane_tile(y)] - total
        return 0

    lax.fori_loop(0, steps, at_step, 0)
    first = per_space * space - REACH
    ids = lax.broadcasted_iota(jnp.int32, (window, ny), 0) + first
    acc = jnp.zeros((window, LANES), F32)
    for x in range(rows):
        hit = jnp.where(ids == patch_ref[x : x + 1, :], weight[x : x + 1, :], 0.0)
        acc = acc + jnp.dot(
            hit, mode_ref[x], precision=lax.Precision.HIGHEST, preferred_element_type=F32
        )
    send_ref[...] = jnp.zeros_like(send_ref)
    first_owner = n_inst * space - REACH // PATCH_DEV
    for j in range(window // PATCH_DEV):
        owner = first_owner + j

        @pl.when((owner >= 0) & (owner < owners))
        def _():
            send_ref[owner] = acc[j * PATCH_DEV : (j + 1) * PATCH_DEV]


def call(kernel, outs, scratch=(), **kwargs):
    return pl.pallas_call(
        kernel,
        out_shape=[jax.ShapeDtypeStruct(shape, F32) for shape in outs],
        scratch_shapes=[pltpu.VMEM(shape, F32) for shape in scratch],
        **kwargs,
    )


def make_body(n_inst, n_space):
    def exchange(chunks):
        return [chunks[0]] + [
            lax.ppermute(chunks[r], "inst", [(i, i ^ r) for i in range(n_inst)])
            for r in range(1, n_inst)
        ]

    def edges(first, last):
        ring = [(i, (i + 1) % n_space) for i in range(n_space)]
        before = lax.ppermute(last, "space", ring)
        after = lax.ppermute(first, "space", [(j, i) for i, j in ring])
        return before, after

    def body(start, source, diagonal, flux_x, flux_y, shape_derivative, mode_basis, patch_of_cell):
        steps, nv, rows, ny = start.shape
        part = nv * (ny // LANES) // n_inst
        chunk = (steps, part, 8, LANES)
        edge = (steps, nv, 8, LANES)
        tile = (nv, rows, ny)

        def per_step(shape):
            return pl.BlockSpec((1,) + shape[1:], lambda t: (t,) + (0,) * (len(shape) - 1))

        def fixed(shape):
            return pl.BlockSpec(shape, lambda t: (0,) * len(shape))

        def bound(kernel, *args):
            def run(*refs):
                kernel(*args, *refs)

            return run

        sweep_specs = [
            per_step(start.shape), per_step(edge), per_step(edge), per_step(source.shape),
            fixed(diagonal.shape), per_step(flux_x.shape), per_step(flux_y.shape),
        ]

        *chunks, first, last = call(
            bound(pack_kernel, n_inst), [chunk] * n_inst + [edge] * 2, name="pack"
        )(start)
        start_cells = exchange(chunks)
        before, after = edges(first, last)
        b = call(
            bound(first_sweep_kernel, n_inst), [chunk] * n_inst,
            scratch=[(nv * ny // LANES, 8, LANES), tile, tile, tile, tile],
            grid=(steps,), in_specs=sweep_specs, out_specs=[per_step(chunk)] * n_inst,
            name="sweep1",
        )(start, before, after, source, diagonal, flux_x, flux_y)
        b_cells = exchange(b)
        z0_cells = call(
            bound(spectral_kernel, n_inst, False), [chunk] * n_inst, scratch=[(NT, 8, LANES)],
            name="spectral1",
        )(diagonal, *start_cells)
        z0 = exchange(z0_cells)
        z1_cells = call(
            bound(spectral_kernel, n_inst, True), [chunk] * n_inst, scratch=[(NT, 8, LANES)],
            name="spectral2",
        )(diagonal, *b_cells, *z0_cells)
        z1 = exchange(z1_cells)
        a1, first, last = call(
            bound(join_kernel, n_inst), [start.shape, edge, edge], name="join"
        )(*b, *z0)
        before, after = edges(first, last)
        x, weight = call(
            second_sweep_kernel, [start.shape, (rows, ny)], scratch=[tile] * 4,
            grid=(steps,), in_specs=sweep_specs + [per_step(shape_derivative.shape)],
            out_specs=[per_step(start.shape), fixed((rows, ny))],
            name="sweep2",
        )(a1, before, after, source, diagonal, flux_x, flux_y, shape_derivative)
        owners = n_inst * n_space
        adjoint, sends = call(
            bound(last_kernel, n_inst), [start.shape, (owners, PATCH_DEV, LANES)],
            scratch=[(rows, ny)], name="last",
        )(x, weight, shape_derivative, mode_basis, patch_of_cell, *z1)
        parts = lax.all_to_all(sends, ("inst", "space"), 0, 0, tiled=True)
        return adjoint, jnp.sum(parts, axis=0)

    return body


def solution(mesh):
    placed = (
        P("inst", None, "space", None),
        P("inst", None, "space", None),
        P(None, "space", None),
        P("inst", None, None, "space", None),
        P("inst", None, None, "space", None),
        P("inst", None, "space", None),
        P("space", None, None),
        P("space", None),
    )
    return jax.shard_map(
        make_body(mesh.shape["inst"], mesh.shape["space"]),
        mesh=mesh,
        in_specs=placed,
        out_specs=(P("inst", None, "space", None), P(("inst", "space"), None)),
        check_vma=False,
    )
```

```python
import math

import jax
import jax.numpy as jnp
import numpy as np
from jax import lax
from jax.experimental import pallas as pl
from jax.experimental.pallas import tpu as pltpu
from jax.sharding import PartitionSpec as P

NT = 32
PATCH_DEV = 8
REACH = 16
LANES = 128
SCALE = 0.1
F32 = jnp.float32
SCRATCH_LIMIT = 4 << 20


def weight_matrix(count):
    weights = np.zeros((count, count))
    for s in range(count):
        for t in range(count):
            if s != t:
                angle = math.pi * (s - t) / count
                weights[s, t] = 0.5 * (-1.0) ** (s - t) * math.cos(angle) / math.sin(angle)
    return weights


def circulant_apply(values):
    count = len(values)
    row = weight_matrix(count)[:, 0]
    if count == 2:
        return None
    half = count // 2
    total = [values[s] + values[s + half] for s in range(half)]
    diff = [values[s] - values[s + half] for s in range(half)]
    even = circulant_apply(total)
    q = [(row[d] - row[d + half]) / 2 for d in range(half)]
    quarter = half // 2

    def at(position):
        position %= count
        return (diff[position], 1.0) if position < half else (diff[position - half], -1.0)

    out = [None] * count
    for t in range(half):
        acc = None
        for d in range(1, quarter):
            plus, sign_plus = at(t + d)
            minus, sign_minus = at(t - d)
            pair = plus - minus if sign_plus == sign_minus else plus + minus
            term = float(q[d] * sign_plus) * pair
            acc = term if acc is None else acc + term
        last, sign = at(t + quarter)
        term = float(q[quarter] * sign) * last
        acc = term if acc is None else acc + term
        if even is None:
            out[t], out[t + half] = acc, -acc
        else:
            out[t], out[t + half] = even[t] + acc, even[t] - acc
    return out


def chunk_place(chunk, n_inst, nv, ny):
    split = n_inst // (ny // LANES)
    return (chunk // split, (chunk % split) * (nv // split)) if split > 1 else (chunk, 0)


def lane_tile(index):
    return pl.ds(pl.multiple_of(index * LANES, LANES), LANES)


def pack_rows(row_block, first_row, ny):
    tiles = ny // LANES
    sub = lax.broadcasted_iota(jnp.int32, (8, LANES), 0)
    packed = None
    for y in range(tiles):
        tile = row_block[:, y * LANES : (y + 1) * LANES]
        shift = (2 * y - first_row) % 8
        moved = pltpu.roll(tile, shift, 0) if shift else tile
        packed = moved if packed is None else jnp.where(sub >= 2 * y, moved, packed)
    return packed


def pack_kernel(n_inst, a_hbm, a_ref, *refs):
    chunks, (first_ref, last_ref, arrived) = refs[:n_inst], refs[n_inst:]
    steps, nv, _, ny = a_ref.shape
    me = lax.axis_index("inst")

    def copy(t):
        return pltpu.make_async_copy(a_hbm.at[t], a_ref.at[t], arrived.at[t])

    for t in range(steps):
        copy(t).start()

    def at_step(t, _):
        copy(t).wait()
        for r in range(n_inst):
            y, k0 = chunk_place(me ^ r, n_inst, nv, ny)
            for k in range(chunks[0].shape[1]):
                chunks[r][t, k] = a_ref[t, k0 + k, :, lane_tile(y)]
        pack_edges(t, a_ref, first_ref, last_ref)
        return 0

    lax.fori_loop(0, steps, at_step, 0)


def pack_edges(t, a_ref, first_ref, last_ref):
    _, nv, _, ny = a_ref.shape
    for k in range(nv):
        rows = a_ref[t, k]
        first_ref[t, k] = pack_rows(rows, 0, ny)
        last_ref[t, k] = pack_rows(rows, 6, ny)


def chord_terms(t, a_ref, src_ref, fy_ref, acc_ref, chord):
    _, nv, rows, ny = a_ref.shape
    lane = lax.broadcasted_iota(jnp.int32, (rows, ny), 1)
    for k in range(nv):
        a = a_ref[t, k]
        above = jnp.where(lane == ny - 1, 0.0, pltpu.roll(a, ny - 1, 1))
        below = jnp.where(lane == 0, 0.0, pltpu.roll(a, 1, 1))
        chord[k] = above - below
        acc_ref[t, k] = src_ref[t, k] + (above + below)
    for y in range(ny // LANES):
        lanes = slice(y * LANES, (y + 1) * LANES)
        tiles = [chord[j, :, lanes] for j in range(nv)]
        for k in range(nv):
            total = fy_ref[t, 0, k, :, lanes] * tiles[0]
            for j in range(1, nv):
                total = total + fy_ref[t, j, k, :, lanes] * tiles[j]
            acc_ref[t, k, :, lanes] = acc_ref[t, k, :, lanes] - total


def first_chord_kernel(
    a_ref, src_hbm, d_hbm, fx_hbm, fy_hbm,
    acc_ref, src_ref, inverse, fx_ref, fy_ref, chord, d_ref, arrived, d_arrived,
):
    steps = a_ref.shape[0]

    pairs = ((src_hbm, src_ref), (fy_hbm, fy_ref), (fx_hbm, fx_ref))

    def copy(i, t):
        there, here = pairs[i]
        return pltpu.make_async_copy(there.at[t], here.at[t], arrived.at[i, t])

    d_copy = pltpu.make_async_copy(d_hbm, d_ref, d_arrived)
    for t in range(steps):
        copy(0, t).start()
        copy(1, t).start()
    d_copy.start()
    for t in range(steps):
        copy(2, t).start()

    def at_step(t, _):
        copy(0, t).wait()
        copy(1, t).wait()
        chord_terms(t, a_ref, src_ref, fy_ref, acc_ref, chord)
        return 0

    lax.fori_loop(0, steps, at_step, 0)
    d_copy.wait()
    inverse[...] = 1.0 / d_ref[...]
    for t in range(steps):
        copy(2, t).wait()


def second_chord_kernel(a_ref, src_ref, fy_ref, acc_ref, chord):
    def at_step(t, _):
        chord_terms(t, a_ref, src_ref, fy_ref, acc_ref, chord)
        return 0

    lax.fori_loop(0, a_ref.shape[0], at_step, 0)


def pitch_terms(t, a_ref, prev_ref, next_ref, pitch, near):
    nv, rows, ny = pitch.shape
    tiles = ny // LANES
    sub = lax.broadcasted_iota(jnp.int32, (rows, LANES), 0)
    for k in range(nv):
        before, after = prev_ref[t, k], next_ref[t, k]
        for y in range(tiles):
            lanes = slice(y * LANES, (y + 1) * LANES)
            a = a_ref[t, k, :, lanes]
            low = pltpu.roll(before, (-2 * y) % 8, 0) if y else before
            high = pltpu.roll(after, (6 - 2 * y) % 8, 0) if (6 - 2 * y) % 8 else after
            edge = jnp.where(sub < 4, low, high)
            plus_two = jnp.where(sub >= 6, edge, pltpu.roll(a, 6, 0))
            plus_one = jnp.where(sub == 7, pltpu.roll(edge, 1, 0), pltpu.roll(a, 7, 0))
            minus_two = jnp.where(sub < 2, edge, pltpu.roll(a, 2, 0))
            minus_one = jnp.where(sub == 0, pltpu.roll(edge, 7, 0), pltpu.roll(a, 1, 0))
            pitch[k, :, lanes] = (
                2.0 / 3.0 * (plus_one - minus_one) - 1.0 / 12.0 * (plus_two - minus_two)
            )
            near[k, :, lanes] = plus_one + minus_one


def swept_tile(t, k, lanes, acc_ref, fx_ref, pitch_tiles, near, inverse):
    total = acc_ref[t, k, :, lanes] + near[k, :, lanes]
    for j in range(len(pitch_tiles)):
        total = total - fx_ref[t, j, k, :, lanes] * pitch_tiles[j]
    return total * inverse[k, :, lanes]


def first_pitch_kernel(n_inst, a_ref, prev_ref, next_ref, acc_ref, fx_ref, inverse, *refs):
    out_refs, (pitch, near) = refs[:n_inst], refs[n_inst:]
    nv, _, ny = pitch.shape
    part = out_refs[0].shape[1]
    me = lax.axis_index("inst")

    def at_step(t, _):
        pitch_terms(t, a_ref, prev_ref, next_ref, pitch, near)
        for r in range(n_inst):
            y, k0 = chunk_place(me ^ r, n_inst, nv, ny)
            lanes = lane_tile(y)
            pitch_tiles = [pitch[j, :, lanes] for j in range(nv)]
            for k in range(part):
                out_refs[r][t, k] = swept_tile(
                    t, k0 + k, lanes, acc_ref, fx_ref, pitch_tiles, near, inverse
                )
        return 0

    lax.fori_loop(0, a_ref.shape[0], at_step, 0)


def spectral_kernel(n_inst, second, inverse, *refs):
    in_refs = refs[:n_inst]
    shift_refs = refs[n_inst : 2 * n_inst] if second else ()
    out_refs = refs[(2 if second else 1) * n_inst : (3 if second else 2) * n_inst]
    (work,) = refs[(3 if second else 2) * n_inst :]
    per, part = in_refs[0].shape[:2]
    nv, _, ny = inverse.shape
    me = lax.axis_index("inst")
    y, k0 = chunk_place(me, n_inst, nv, ny)

    def at_tile(c, _):
        for r in range(n_inst):
            base = (me ^ r) * per
            for t in range(per):
                value = in_refs[r][t, c]
                if second:
                    value = value - shift_refs[r][t, c]
                work[base + t] = value
        out = circulant_apply([work[s] for s in range(NT)])
        factor = SCALE * inverse[k0 + c, :, lane_tile(y)]
        for s in range(NT):
            work[s] = out[s] * factor
        for r in range(n_inst):
            base = (me ^ r) * per
            for t in range(per):
                out_refs[r][t, c] = work[base + t]
        return 0

    lax.fori_loop(0, part, at_tile, 0)


def join_kernel(n_inst, *refs):
    b_refs, z_refs = refs[:n_inst], refs[n_inst : 2 * n_inst]
    a_ref, first_ref, last_ref = refs[2 * n_inst :]
    steps, nv, _, ny = a_ref.shape
    me = lax.axis_index("inst")

    def at_step(t, _):
        for r in range(n_inst):
            y, k0 = chunk_place(me ^ r, n_inst, nv, ny)
            for k in range(b_refs[0].shape[1]):
                a_ref[t, k0 + k, :, lane_tile(y)] = b_refs[r][t, k] - z_refs[r][t, k]
        pack_edges(t, a_ref, first_ref, last_ref)
        return 0

    lax.fori_loop(0, steps, at_step, 0)


def second_pitch_kernel(
    a_ref, prev_ref, next_ref, acc_ref, fx_ref, inverse, shape_ref, out_ref, weight_ref, pitch, near
):
    nv, _, ny = pitch.shape
    weight_ref[...] = jnp.zeros_like(weight_ref)

    def at_step(t, _):
        pitch_terms(t, a_ref, prev_ref, next_ref, pitch, near)
        for y in range(ny // LANES):
            lanes = slice(y * LANES, (y + 1) * LANES)
            pitch_tiles = [pitch[j, :, lanes] for j in range(nv)]
            weight = weight_ref[:, lanes]
            for k in range(nv):
                value = swept_tile(t, k, lanes, acc_ref, fx_ref, pitch_tiles, near, inverse)
                out_ref[t, k, :, lanes] = value
                weight = weight + value * shape_ref[t, k, :, lanes]
            weight_ref[:, lanes] = weight
        return 0

    lax.fori_loop(0, a_ref.shape[0], at_step, 0)


def last_kernel(n_inst, x_ref, weight_ref, shape_ref, mode_ref, patch_ref, *refs):
    z_refs, (a_ref, send_ref, weight) = refs[:n_inst], refs[n_inst:]
    steps, nv, rows, ny = x_ref.shape
    part = z_refs[0].shape[1]
    me, space = lax.axis_index("inst"), lax.axis_index("space")
    owners = send_ref.shape[0]
    per_space = PATCH_DEV * n_inst
    window = per_space + 2 * REACH
    weight[...] = weight_ref[...]

    def at_step(t, _):
        for r in range(n_inst):
            y, k0 = chunk_place(me ^ r, n_inst, nv, ny)
            total = jnp.zeros((rows, LANES), F32)
            for k in range(part):
                z = z_refs[r][t, k]
                a_ref[t, k0 + k, :, lane_tile(y)] = (
                    x_ref[t, k0 + k, :, lane_tile(y)] - z
                )
                total = total + z * shape_ref[t, k0 + k, :, lane_tile(y)]
            weight[:, lane_tile(y)] = weight[:, lane_tile(y)] - total
        return 0

    lax.fori_loop(0, steps, at_step, 0)
    first = per_space * space - REACH
    ids = lax.broadcasted_iota(jnp.int32, (window, ny), 0) + first
    acc = jnp.zeros((window, LANES), F32)
    for x in range(rows):
        hit = jnp.where(ids == patch_ref[x : x + 1, :], weight[x : x + 1, :], 0.0)
        acc = acc + jnp.dot(
            hit, mode_ref[x], precision=lax.Precision.HIGHEST, preferred_element_type=F32
        )
    send_ref[...] = jnp.zeros_like(send_ref)
    first_owner = n_inst * space - REACH // PATCH_DEV
    for j in range(window // PATCH_DEV):
        owner = first_owner + j

        @pl.when((owner >= 0) & (owner < owners))
        def _():
            send_ref[owner] = acc[j * PATCH_DEV : (j + 1) * PATCH_DEV]


def call(kernel, outs, scratch=(), n_hbm=None, name=None):
    n_hbm = n_hbm or ()
    scratch_shapes = [pltpu.VMEM(x, F32) if isinstance(x, tuple) else x for x in scratch]

    def run(*args):
        return pl.pallas_call(
            kernel,
            out_shape=[pltpu.VMEM(shape, F32) for shape in outs],
            in_specs=[
                pl.BlockSpec(memory_space=pltpu.HBM if i in n_hbm else pltpu.VMEM)
                for i in range(len(args))
            ],
            scratch_shapes=scratch_shapes,
            compiler_params=pltpu.CompilerParams(vmem_limit_bytes=SCRATCH_LIMIT),
            name=name,
        )(
            *(
                pltpu.with_memory_space_constraint(x, pltpu.HBM if i in n_hbm else pltpu.VMEM)
                for i, x in enumerate(args)
            )
        )

    return run


def make_body(n_inst, n_space):
    def exchange(chunks):
        return [chunks[0]] + [
            lax.ppermute(chunks[r], "inst", [(i, i ^ r) for i in range(n_inst)])
            for r in range(1, n_inst)
        ]

    def edges(first, last):
        ring = [(i, (i + 1) % n_space) for i in range(n_space)]
        before = lax.ppermute(last, "space", ring)
        after = lax.ppermute(first, "space", [(j, i) for i, j in ring])
        return before, after

    def body(start, source, diagonal, flux_x, flux_y, shape_derivative, mode_basis, patch_of_cell):
        steps, nv, rows, ny = start.shape
        part = nv * (ny // LANES) // n_inst
        chunk = (steps, part, 8, LANES)
        edge = (steps, nv, 8, LANES)
        tile = (nv, rows, ny)

        def bound(kernel, *args):
            def run(*refs):
                kernel(*args, *refs)

            return run

        a0, *chunks, first, last = call(
            bound(pack_kernel, n_inst), [start.shape] + [chunk] * n_inst + [edge] * 2,
            scratch=[pltpu.SemaphoreType.DMA((steps,))], n_hbm=(0,), name="pack",
        )(start)
        before, after = edges(first, last)
        start_cells = exchange(chunks)
        acc, src, inverse, fx, fy = call(
            first_chord_kernel,
            [start.shape, source.shape, tile, flux_x.shape, flux_y.shape],
            scratch=[
                tile, tile, pltpu.SemaphoreType.DMA((3, steps)), pltpu.SemaphoreType.DMA(())
            ],
            n_hbm=(1, 2, 3, 4), name="chord1",
        )(a0, source, diagonal, flux_x, flux_y)
        b = call(
            bound(first_pitch_kernel, n_inst), [chunk] * n_inst, scratch=[tile, tile], name="pitch1"
        )(a0, before, after, acc, fx, inverse)
        b_cells = exchange(b)
        z0_cells = call(
            bound(spectral_kernel, n_inst, False), [chunk] * n_inst, scratch=[(NT, 8, LANES)],
            name="spectral1",
        )(inverse, *start_cells)
        z0 = exchange(z0_cells)
        z1_cells = call(
            bound(spectral_kernel, n_inst, True), [chunk] * n_inst, scratch=[(NT, 8, LANES)],
            name="spectral2",
        )(inverse, *b_cells, *z0_cells)
        z1 = exchange(z1_cells)
        a1, first, last = call(
            bound(join_kernel, n_inst), [start.shape, edge, edge], name="join"
        )(*b, *z0)
        before, after = edges(first, last)
        (acc,) = call(second_chord_kernel, [start.shape], scratch=[tile], name="chord2")(
            a1, src, fy
        )
        x, weight = call(
            second_pitch_kernel, [start.shape, (rows, ny)], scratch=[tile, tile], name="pitch2"
        )(a1, before, after, acc, fx, inverse, shape_derivative)
        owners = n_inst * n_space
        adjoint, sends = call(
            bound(last_kernel, n_inst), [start.shape, (owners, PATCH_DEV, LANES)],
            scratch=[(rows, ny)], name="last",
        )(x, weight, shape_derivative, mode_basis, patch_of_cell, *z1)
        parts = lax.all_to_all(sends, ("inst", "space"), 0, 0, tiled=True)
        return adjoint, jnp.sum(parts, axis=0)

    return body


def solution(mesh):
    placed = (
        P("inst", None, "space", None),
        P("inst", None, "space", None),
        P(None, "space", None),
        P("inst", None, None, "space", None),
        P("inst", None, None, "space", None),
        P("inst", None, "space", None),
        P("space", None, None),
        P("space", None),
    )
    return jax.shard_map(
        make_body(mesh.shape["inst"], mesh.shape["space"]),
        mesh=mesh,
        in_specs=placed,
        out_specs=(P("inst", None, "space", None), P(("inst", "space"), None)),
        check_vma=False,
    )
```

```python
import math

import jax
import jax.numpy as jnp
import numpy as np
from jax import lax
from jax.experimental import pallas as pl
from jax.experimental.pallas import tpu as pltpu
from jax.sharding import PartitionSpec as P

NT = 32
PATCH_DEV = 8
REACH = 16
LANES = 128
SCALE = 0.1
F32 = jnp.float32
SCRATCH_LIMIT = 4 << 20


def weight_matrix(count):
    weights = np.zeros((count, count))
    for s in range(count):
        for t in range(count):
            if s != t:
                angle = math.pi * (s - t) / count
                weights[s, t] = 0.5 * (-1.0) ** (s - t) * math.cos(angle) / math.sin(angle)
    return weights


def circulant_apply(values):
    count = len(values)
    row = weight_matrix(count)[:, 0]
    if count == 2:
        return None
    half = count // 2
    total = [values[s] + values[s + half] for s in range(half)]
    diff = [values[s] - values[s + half] for s in range(half)]
    even = circulant_apply(total)
    q = [(row[d] - row[d + half]) / 2 for d in range(half)]
    quarter = half // 2

    def at(position):
        position %= count
        return (diff[position], 1.0) if position < half else (diff[position - half], -1.0)

    out = [None] * count
    for t in range(half):
        acc = None
        for d in range(1, quarter):
            plus, sign_plus = at(t + d)
            minus, sign_minus = at(t - d)
            pair = plus - minus if sign_plus == sign_minus else plus + minus
            term = float(q[d] * sign_plus) * pair
            acc = term if acc is None else acc + term
        last, sign = at(t + quarter)
        term = float(q[quarter] * sign) * last
        acc = term if acc is None else acc + term
        if even is None:
            out[t], out[t + half] = acc, -acc
        else:
            out[t], out[t + half] = even[t] + acc, even[t] - acc
    return out


def chunk_place(chunk, n_inst, nv, ny):
    split = n_inst // (ny // LANES)
    return (chunk // split, (chunk % split) * (nv // split)) if split > 1 else (chunk, 0)


def lane_tile(index):
    return pl.ds(pl.multiple_of(index * LANES, LANES), LANES)


def pack_rows(row_block, first_row, ny):
    tiles = ny // LANES
    sub = lax.broadcasted_iota(jnp.int32, (8, LANES), 0)
    packed = None
    for y in range(tiles):
        tile = row_block[:, y * LANES : (y + 1) * LANES]
        shift = (2 * y - first_row) % 8
        moved = pltpu.roll(tile, shift, 0) if shift else tile
        packed = moved if packed is None else jnp.where(sub >= 2 * y, moved, packed)
    return packed


def pack_kernel(n_inst, a_hbm, a_ref, *refs):
    chunks, (arrived,) = refs[:n_inst], refs[n_inst:]
    steps, nv, _, ny = a_ref.shape
    me = lax.axis_index("inst")

    def copy(t):
        return pltpu.make_async_copy(a_hbm.at[t], a_ref.at[t], arrived.at[t])

    for t in range(steps):
        copy(t).start()

    def at_step(t, _):
        copy(t).wait()
        for r in range(n_inst):
            y, k0 = chunk_place(me ^ r, n_inst, nv, ny)
            for k in range(chunks[0].shape[1]):
                chunks[r][t, k] = a_ref[t, k0 + k, :, lane_tile(y)]
        return 0

    lax.fori_loop(0, steps, at_step, 0)


def edges_kernel(a_ref, first_ref, last_ref):
    def at_step(t, _):
        pack_edges(t, a_ref, first_ref, last_ref)
        return 0

    lax.fori_loop(0, a_ref.shape[0], at_step, 0)


def pack_edges(t, a_ref, first_ref, last_ref):
    _, nv, _, ny = a_ref.shape
    for k in range(nv):
        rows = a_ref[t, k]
        first_ref[t, k] = pack_rows(rows, 0, ny)
        last_ref[t, k] = pack_rows(rows, 6, ny)


def chord_terms(t, a_ref, src_ref, fy_ref, acc_ref, chord):
    _, nv, rows, ny = a_ref.shape
    lane = lax.broadcasted_iota(jnp.int32, (rows, ny), 1)
    for k in range(nv):
        a = a_ref[t, k]
        above = jnp.where(lane == ny - 1, 0.0, pltpu.roll(a, ny - 1, 1))
        below = jnp.where(lane == 0, 0.0, pltpu.roll(a, 1, 1))
        chord[k] = above - below
        acc_ref[t, k] = src_ref[t, k] + (above + below)
    for y in range(ny // LANES):
        lanes = slice(y * LANES, (y + 1) * LANES)
        tiles = [chord[j, :, lanes] for j in range(nv)]
        for k in range(nv):
            total = fy_ref[t, 0, k, :, lanes] * tiles[0]
            for j in range(1, nv):
                total = total + fy_ref[t, j, k, :, lanes] * tiles[j]
            acc_ref[t, k, :, lanes] = acc_ref[t, k, :, lanes] - total


def first_chord_kernel(
    a_ref, src_hbm, d_hbm, fy_hbm, acc_ref, src_ref, inverse, fy_ref, chord, d_ref, arrived, d_arrived
):
    steps = a_ref.shape[0]
    pairs = ((src_hbm, src_ref), (fy_hbm, fy_ref))

    def copy(i, t):
        there, here = pairs[i]
        return pltpu.make_async_copy(there.at[t], here.at[t], arrived.at[i, t])

    d_copy = pltpu.make_async_copy(d_hbm, d_ref, d_arrived)
    for t in range(steps):
        copy(0, t).start()
        copy(1, t).start()
    d_copy.start()

    def at_step(t, _):
        copy(0, t).wait()
        copy(1, t).wait()
        chord_terms(t, a_ref, src_ref, fy_ref, acc_ref, chord)
        return 0

    lax.fori_loop(0, steps, at_step, 0)
    d_copy.wait()
    inverse[...] = 1.0 / d_ref[...]


def second_chord_kernel(a_ref, src_ref, fy_ref, acc_ref, chord):
    def at_step(t, _):
        chord_terms(t, a_ref, src_ref, fy_ref, acc_ref, chord)
        return 0

    lax.fori_loop(0, a_ref.shape[0], at_step, 0)


def pitch_terms(t, a_ref, prev_ref, next_ref, pitch, near):
    nv, rows, ny = pitch.shape
    tiles = ny // LANES
    sub = lax.broadcasted_iota(jnp.int32, (rows, LANES), 0)
    for k in range(nv):
        before, after = prev_ref[t, k], next_ref[t, k]
        for y in range(tiles):
            lanes = slice(y * LANES, (y + 1) * LANES)
            a = a_ref[t, k, :, lanes]
            low = pltpu.roll(before, (-2 * y) % 8, 0) if y else before
            high = pltpu.roll(after, (6 - 2 * y) % 8, 0) if (6 - 2 * y) % 8 else after
            edge = jnp.where(sub < 4, low, high)
            plus_two = jnp.where(sub >= 6, edge, pltpu.roll(a, 6, 0))
            plus_one = jnp.where(sub == 7, pltpu.roll(edge, 1, 0), pltpu.roll(a, 7, 0))
            minus_two = jnp.where(sub < 2, edge, pltpu.roll(a, 2, 0))
            minus_one = jnp.where(sub == 0, pltpu.roll(edge, 7, 0), pltpu.roll(a, 1, 0))
            pitch[k, :, lanes] = (
                2.0 / 3.0 * (plus_one - minus_one) - 1.0 / 12.0 * (plus_two - minus_two)
            )
            near[k, :, lanes] = plus_one + minus_one


def swept_tile(t, k, lanes, acc_ref, fx_ref, pitch_tiles, near, inverse):
    total = acc_ref[t, k, :, lanes] + near[k, :, lanes]
    for j in range(len(pitch_tiles)):
        total = total - fx_ref[t, j, k, :, lanes] * pitch_tiles[j]
    return total * inverse[k, :, lanes]


def first_pitch_kernel(n_inst, a_ref, prev_ref, next_ref, acc_ref, fx_hbm, inverse, *refs):
    out_refs, (fx_ref, pitch, near, arrived) = refs[:n_inst], refs[n_inst:]
    nv, _, ny = pitch.shape
    part = out_refs[0].shape[1]
    me = lax.axis_index("inst")

    def copy(t):
        return pltpu.make_async_copy(fx_hbm.at[t], fx_ref.at[t], arrived.at[t])

    for t in range(a_ref.shape[0]):
        copy(t).start()

    def at_step(t, _):
        pitch_terms(t, a_ref, prev_ref, next_ref, pitch, near)
        copy(t).wait()
        for r in range(n_inst):
            y, k0 = chunk_place(me ^ r, n_inst, nv, ny)
            lanes = lane_tile(y)
            pitch_tiles = [pitch[j, :, lanes] for j in range(nv)]
            for k in range(part):
                out_refs[r][t, k] = swept_tile(
                    t, k0 + k, lanes, acc_ref, fx_ref, pitch_tiles, near, inverse
                )
        return 0

    lax.fori_loop(0, a_ref.shape[0], at_step, 0)


def spectral_kernel(n_inst, second, inverse, *refs):
    in_refs, shift_refs = refs[:n_inst], refs[n_inst : 2 * n_inst]
    out_refs, (work,) = refs[2 * n_inst : 3 * n_inst], refs[3 * n_inst :]
    per, part = in_refs[0].shape[:2]
    nv, _, ny = inverse.shape
    me = lax.axis_index("inst")
    y, k0 = chunk_place(me, n_inst, nv, ny)

    def at_tile(c, _):
        for r in range(n_inst):
            base = (me ^ r) * per
            for t in range(per):
                value = in_refs[r][t, c]
                if second:
                    value = value - shift_refs[r][t, c]
                work[base + t] = value
        out = circulant_apply([work[s] for s in range(NT)])
        factor = SCALE * inverse[k0 + c, :, lane_tile(y)]
        for s in range(NT):
            work[s] = out[s] * factor
        for r in range(n_inst):
            base = (me ^ r) * per
            for t in range(per):
                out_refs[r][t, c] = work[base + t]
        return 0

    lax.fori_loop(0, part, at_tile, 0)


def join_kernel(n_inst, *refs):
    b_refs, z_refs = refs[:n_inst], refs[n_inst : 2 * n_inst]
    a_ref, first_ref, last_ref = refs[-3:]
    steps, nv, _, ny = a_ref.shape
    me = lax.axis_index("inst")

    def at_step(t, _):
        for r in range(n_inst):
            y, k0 = chunk_place(me ^ r, n_inst, nv, ny)
            for k in range(b_refs[0].shape[1]):
                a_ref[t, k0 + k, :, lane_tile(y)] = b_refs[r][t, k] - z_refs[r][t, k]
        pack_edges(t, a_ref, first_ref, last_ref)
        return 0

    lax.fori_loop(0, steps, at_step, 0)


def second_pitch_kernel(
    a_ref, prev_ref, next_ref, acc_ref, fx_ref, inverse, shape_ref, out_ref, weight_ref, pitch, near
):
    nv, _, ny = pitch.shape
    weight_ref[...] = jnp.zeros_like(weight_ref)

    def at_step(t, _):
        pitch_terms(t, a_ref, prev_ref, next_ref, pitch, near)
        for y in range(ny // LANES):
            lanes = slice(y * LANES, (y + 1) * LANES)
            pitch_tiles = [pitch[j, :, lanes] for j in range(nv)]
            weight = weight_ref[:, lanes]
            for k in range(nv):
                value = swept_tile(t, k, lanes, acc_ref, fx_ref, pitch_tiles, near, inverse)
                out_ref[t, k, :, lanes] = value
                weight = weight + value * shape_ref[t, k, :, lanes]
            weight_ref[:, lanes] = weight
        return 0

    lax.fori_loop(0, a_ref.shape[0], at_step, 0)


def basis_kernel(mode_ref, _, split_ref):
    def at_row(x, _):
        mode = mode_ref[x]
        high = mode.astype(jnp.bfloat16)
        split_ref[x, :, :LANES] = high
        split_ref[x, :, LANES:] = (mode - high.astype(F32)).astype(jnp.bfloat16)
        return 0

    lax.fori_loop(0, mode_ref.shape[0], at_row, 0)


def weight_kernel(n_inst, x_weight_ref, shape_ref, *refs):
    z_refs, (weight,) = refs[:n_inst], refs[n_inst:]
    steps, nv, _, ny = shape_ref.shape
    me = lax.axis_index("inst")
    weight[...] = x_weight_ref[...]
    for r in range(n_inst):
        y, k0 = chunk_place(me ^ r, n_inst, nv, ny)
        lanes = lane_tile(y)

        def at_step(t, total):
            for k in range(z_refs[0].shape[1]):
                total = total - z_refs[r][t, k] * shape_ref[t, k0 + k, :, lanes]
            return total

        weight[:, lanes] = lax.fori_loop(0, steps, at_step, weight[:, lanes])


def own_block(inst, space, n_inst, n_space, choose):
    first = n_inst * space
    apart = inst ^ (first // n_space)
    to_first = abs(first % n_space - space)
    to_last = abs(first % n_space + n_inst - 1 - space)
    return choose(to_first >= to_last, apart, n_inst - 1 - apart)


def sums_kernel(n_inst, n_space, split_ref, patch_ref, *refs):
    weight_refs, (block_ref, beyond_ref, blocks) = refs[:n_inst], refs[n_inst:]
    rows, ny = patch_ref.shape
    me, space = lax.axis_index("inst"), lax.axis_index("space")
    over = REACH // PATCH_DEV
    per_space = PATCH_DEV * n_inst
    window = per_space + 2 * REACH
    weight = weight_refs[0][...]
    for other in weight_refs[1:]:
        weight = weight + other[...]
    ids = lax.broadcasted_iota(jnp.int32, (window, ny), 0) + (per_space * space - REACH)
    acc = jnp.zeros((window, LANES), F32)
    for x in range(rows):
        row = weight[x : x + 1, :]
        high = row.astype(jnp.bfloat16).astype(F32)
        hit = ids == patch_ref[x : x + 1, :]
        factors = jnp.concatenate(
            [
                jnp.where(hit, high, 0.0).astype(jnp.bfloat16),
                jnp.where(hit, row - high, 0.0).astype(jnp.bfloat16),
            ],
            axis=0,
        )
        product = jnp.dot(factors, split_ref[x], preferred_element_type=F32)
        acc = acc + (
            (product[:window, :LANES] + product[window:, :LANES])
            + (product[:window, LANES:] + product[window:, LANES:])
        )
    for j in range(window // PATCH_DEV):
        blocks[j] = acc[j * PATCH_DEV : (j + 1) * PATCH_DEV]
    block_ref[...] = blocks[over + own_block(me, space, n_inst, n_space, jnp.where)]
    side = jnp.minimum(me, 2 * over - 1)
    beyond_ref[...] = blocks[jnp.where(side < over, side, side + n_inst)]


def adjoint_kernel(n_inst, x_ref, _, *refs):
    z_refs, (out_hbm, a_ref, left) = refs[:n_inst], refs[n_inst:]
    steps, nv, _, ny = x_ref.shape
    me = lax.axis_index("inst")

    def copy(t):
        return pltpu.make_async_copy(a_ref.at[t], out_hbm.at[t], left.at[t])

    def at_step(t, _):
        for r in range(n_inst):
            y, k0 = chunk_place(me ^ r, n_inst, nv, ny)
            for k in range(z_refs[0].shape[1]):
                a_ref[t, k0 + k, :, lane_tile(y)] = (
                    x_ref[t, k0 + k, :, lane_tile(y)] - z_refs[r][t, k]
                )
        copy(t).start()
        return 0

    lax.fori_loop(0, steps, at_step, 0)
    for t in range(steps):
        copy(t).wait()


def total_kernel(block_ref, beyond_ref, out_ref):
    out_ref[...] = block_ref[...] + beyond_ref[...]


def call(kernel, outs, scratch=(), n_hbm=None):
    n_hbm = n_hbm or ()
    scratch_shapes = [pltpu.VMEM(x, F32) if isinstance(x, tuple) else x for x in scratch]

    def run(*args):
        return pl.pallas_call(
            kernel,
            out_shape=[pltpu.VMEM(x, F32) if isinstance(x, tuple) else x for x in outs],
            out_specs=[
                pl.BlockSpec(memory_space=pltpu.VMEM if isinstance(x, tuple) else x.memory_space)
                for x in outs
            ],
            in_specs=[
                pl.BlockSpec(memory_space=pltpu.HBM if i in n_hbm else pltpu.VMEM)
                for i in range(len(args))
            ],
            scratch_shapes=scratch_shapes,
            compiler_params=pltpu.CompilerParams(vmem_limit_bytes=SCRATCH_LIMIT),
        )(
            *(
                pltpu.with_memory_space_constraint(x, pltpu.HBM if i in n_hbm else pltpu.VMEM)
                for i, x in enumerate(args)
            )
        )

    return run


def owner_pairs(n_inst, n_space):
    own, beyond = [], []
    over = REACH // PATCH_DEV
    for inst in range(n_inst):
        for space in range(n_space):
            here, first = inst * n_space + space, n_inst * space
            block = own_block(
                inst, space, n_inst, n_space, lambda test, yes, no: yes if test else no
            )
            own.append((here, first + block))
            if inst < 2 * over:
                owner = first + (inst - over if inst < over else n_inst + inst - over)
                if 0 <= owner < n_inst * n_space:
                    beyond.append((here, owner))
    return own, beyond


def make_body(n_inst, n_space):
    def exchange(chunks):
        return [chunks[0]] + [
            lax.ppermute(chunks[r], "inst", [(i, i ^ r) for i in range(n_inst)])
            for r in range(1, n_inst)
        ]

    def edges(first, last):
        ring = [(i, (i + 1) % n_space) for i in range(n_space)]
        before = lax.ppermute(last, "space", ring)
        after = lax.ppermute(first, "space", [(j, i) for i, j in ring])
        return before, after

    def body(start, source, diagonal, flux_x, flux_y, shape_derivative, mode_basis, patch_of_cell):
        steps, nv, rows, ny = start.shape
        part = nv * (ny // LANES) // n_inst
        chunk = (steps, part, 8, LANES)
        edge = (steps, nv, 8, LANES)
        tile = (nv, rows, ny)

        def bound(kernel, *args):
            def run(*refs):
                kernel(*args, *refs)

            return run

        a0, *chunks = call(
            bound(pack_kernel, n_inst), [start.shape] + [chunk] * n_inst,
            scratch=[pltpu.SemaphoreType.DMA((steps,))], n_hbm=(0,),
        )(start)
        start_cells = exchange(chunks)
        first, last = call(edges_kernel, [edge, edge])(a0)
        before, after = edges(first, last)
        acc, src, inverse, fy = call(
            first_chord_kernel, [start.shape, source.shape, tile, flux_y.shape],
            scratch=[
                tile, tile, pltpu.SemaphoreType.DMA((2, steps)), pltpu.SemaphoreType.DMA(())
            ],
            n_hbm=(1, 2, 3),
        )(a0, source, diagonal, flux_y)
        *b, fx = call(
            bound(first_pitch_kernel, n_inst), [chunk] * n_inst + [flux_x.shape],
            scratch=[tile, tile, pltpu.SemaphoreType.DMA((steps,))], n_hbm=(4,),
        )(a0, before, after, acc, flux_x, inverse)
        b_cells = exchange(b)
        z0_cells = call(
            bound(spectral_kernel, n_inst, False), [chunk] * n_inst, scratch=[(NT, 8, LANES)],
        )(inverse, *start_cells, *([acc] * n_inst))
        z0 = exchange(z0_cells)
        z1_cells = call(
            bound(spectral_kernel, n_inst, True), [chunk] * n_inst, scratch=[(NT, 8, LANES)],
        )(inverse, *b_cells, *z0_cells)
        z1 = exchange(z1_cells)
        a1, first, last = call(bound(join_kernel, n_inst), [start.shape, edge, edge])(*b, *z0)
        before, after = edges(first, last)
        (acc,) = call(second_chord_kernel, [start.shape], scratch=[tile])(a1, src, fy)
        x, weight = call(
            second_pitch_kernel, [start.shape, (rows, ny)], scratch=[tile, tile]
        )(a1, before, after, acc, fx, inverse, shape_derivative)
        (split,) = call(
            basis_kernel, [pltpu.VMEM((rows, ny, 2 * LANES), jnp.bfloat16)]
        )(mode_basis, weight)
        (weight,) = call(bound(weight_kernel, n_inst), [(rows, ny)])(weight, shape_derivative, *z1)
        weights = exchange([weight] * n_inst)
        block, beyond = call(
            bound(sums_kernel, n_inst, n_space), [(PATCH_DEV, LANES)] * 2,
            scratch=[(n_inst + 2 * REACH // PATCH_DEV, PATCH_DEV, LANES)],
        )(split, patch_of_cell, *weights)
        block, beyond = (
            lax.ppermute(x, ("inst", "space"), pairs)
            for x, pairs in zip((block, beyond), owner_pairs(n_inst, n_space))
        )
        (adjoint,) = call(
            bound(adjoint_kernel, n_inst), [pltpu.HBM(start.shape, F32)],
            scratch=[start.shape, pltpu.SemaphoreType.DMA((steps,))],
        )(x, weight, *z1)
        (sensitivity,) = call(total_kernel, [(PATCH_DEV, LANES)])(block, beyond)
        return adjoint, sensitivity

    return body


def solution(mesh):
    placed = (
        P("inst", None, "space", None),
        P("inst", None, "space", None),
        P(None, "space", None),
        P("inst", None, None, "space", None),
        P("inst", None, None, "space", None),
        P("inst", None, "space", None),
        P("space", None, None),
        P("space", None),
    )
    n_inst, n_space = mesh.shape["inst"], mesh.shape["space"]
    body = make_body(n_inst, n_space)


    return jax.shard_map(
        body,
        mesh=mesh,
        in_specs=placed,
        out_specs=(P("inst", None, "space", None), P(("inst", "space"), None)),
        check_vma=False,
    )
```
